512 devices in a mesh: tile: 32 (over z, core), tmpl: 16 (over y, x).
Axes of the slice: x: 4, y: 4, z: 16, core: 2. Of those that a mesh axis runs over, the one named last changes fastest.
Arguments:
- sky_image: float32 [10, 512, 2048], P(None, 'tile'), may hold values from -8 to 8
- inverse_var: float32 [10, 512, 2048], P(None, 'tile'), may hold values from 0.3 to 3
- kernel_taps: float32 [10, 17], replicated, may hold values from 0.2 to 1
- kernel_sizes: int32 [10], replicated, may hold values from 1 to 8, as said below
- templates: float32 [10, 2048], P(None, 'tmpl'), may hold values from 0.1 to 10
- grid_index: int32 [3, 2048], P(None, 'tmpl'), may hold values from 0 to 63
Outputs:
- post_means: float32 [3, 512, 2048], P(None, 'tile', 'tmpl')
- log_evidence: float32 [512, 2048], P('tile', 'tmpl')
The draws below stay inside these ranges and needn't reach their ends.
Inputs may be any that keep to these rules, and one draw needn't show every extreme that they name: `kernel_sizes`: some band has half-width 8 and some other band has half-width 1.
All inputs are finite; a program needn't handle non-finite values.
Results may differ from the reference program's by a relative error of at most 0.0003.
Values sent between devices are 32-bit elements; how exact they have to be, the bound alone decides.
No kernel may reach another device: no remote copies, remote signals or barrier semaphores. Data moves between devices by JAX's collectives and lax.ppermute only.
A program may use at most 64 MiB of HBM per device.

```python
import math
import jax
import jax.numpy as jnp
from jax import lax

BANDS = 10
NTMPL = 2048
NCOLS = 2048
RADIUS = 8
GRID = 64
NROWS = 512


def draw_kernel_sizes(key, part):
    first_key, second_key, third_key = jax.random.split(key, 3)
    values = jax.random.randint(first_key, (BANDS,), 1, RADIUS + 1)
    widest = jax.random.randint(second_key, (), 0, BANDS)
    step_on = jax.random.randint(third_key, (), 1, BANDS)
    narrow = (widest + step_on) % BANDS
    places = jnp.arange(BANDS)
    values = jnp.where(places == widest, RADIUS, values)
    values = jnp.where(places == narrow, 1, values)
    return values.astype(jnp.int32)


def draw_sky_image(key, part):
    shape = (BANDS, NROWS, NCOLS)
    noise_key = jax.random.fold_in(key, 1)
    values = jnp.clip(2.0 * jax.random.normal(noise_key, shape, jnp.float32), -8.0, 8.0)
    return values.astype(jnp.float32)


def draw_inverse_var(key, part):
    shape = (BANDS, NROWS, NCOLS)
    spread_key = jax.random.fold_in(key, 3)
    logs = jax.random.uniform(spread_key, shape, jnp.float32, jnp.log(0.3), jnp.log(3.0))
    values = jnp.clip(jnp.exp(logs), 0.3, 3.0)
    return values.astype(jnp.float32)


def place_ends(entries, stream_key, low, top_value):
    longest = entries.shape.index(max(entries.shape))
    spots = []
    for shift in (0, 1):
        where = [jax.random.randint(jax.random.fold_in(stream_key, axis), (), 0, length) for axis, length in enumerate(entries.shape)]
        where[longest] = (where[longest] + shift) % entries.shape[longest]
        spots.append(tuple(where))
    return entries.at[spots[0]].set(low).at[spots[1]].set(top_value)


def block_scale(rng, extent, shards, least, top_value):
    def one(dim, blocks):
        steps = jax.random.uniform(jax.random.fold_in(jax.random.fold_in(rng, 6), dim), (blocks,), jnp.float32, least / len(shards), top_value / len(shards))
        return jnp.repeat(jnp.exp(steps), extent[dim] // blocks).reshape((-1,) + (1,) * (len(extent) - dim - 1))

    factor_of = one(*shards[0])
    for cut in shards[1:]:
        factor_of = factor_of * one(*cut)
    return factor_of


def setup_inputs(seed: int = 0) -> dict:
    key_list = jax.random.split(jax.random.key(seed), 7)
    return {
        "sky_image": draw_sky_image(jax.random.fold_in(key_list[6], 71), 0),
        "inverse_var": draw_inverse_var(jax.random.fold_in(key_list[6], 71), 0),
        "kernel_taps": jnp.clip(jnp.exp(jax.random.uniform(key_list[2], (BANDS, 2 * RADIUS + 1), jnp.float32, math.log(0.2), math.log(1.0))), 0.2, 1.0),
        "kernel_sizes": draw_kernel_sizes(jax.random.fold_in(key_list[6], 71), 0),
        "templates": jnp.clip(jnp.exp(math.log(10.0) - 4.6051702 * jax.random.uniform(key_list[4], (BANDS, NTMPL), jnp.float32) ** block_scale(key_list[4], (BANDS, NTMPL), ((1, 16),), -0.2, 0.2)), 0.1, 10.0),
        "grid_index": place_ends(jax.random.randint(key_list[5], (3, NTMPL), 0, GRID), jax.random.fold_in(key_list[5], 1), 0, GRID - 1).astype(jnp.int32),
    }


def kernel_table(kernel_taps, kernel_sizes):
    offsets = jnp.arange(2 * RADIUS + 1, dtype=jnp.int32) - RADIUS
    inside = jnp.abs(offsets)[None, :] <= kernel_sizes[:, None]
    masked = jnp.where(inside, kernel_taps, jnp.float32(0.0))
    return masked / jnp.sum(masked, axis=1, keepdims=True)


def convolve_rows(padded, kernel, height):
    result = jnp.zeros((padded.shape[0], height, padded.shape[2]), jnp.float32)
    for offset in range(2 * RADIUS + 1):
        result = result + kernel[:, offset, None, None] * padded[:, offset:offset + height, :]
    return result


def convolve_cols(padded, kernel, width):
    result = jnp.zeros((padded.shape[0], padded.shape[1], width), jnp.float32)
    for offset in range(2 * RADIUS + 1):
        result = result + kernel[:, offset, None, None] * padded[:, :, offset:offset + width]
    return result


def fit_pixels(flux, weight, bank, coords):
    bands, pixels = flux.shape
    block = math.gcd(pixels, 2048)
    count = pixels // block
    flux_blocks = flux.reshape(bands, count, block).transpose(1, 0, 2)
    weight_blocks = weight.reshape(bands, count, block).transpose(1, 0, 2)
    squared = bank * bank

    def one_block(pair):
        flux_part, weight_part = pair
        weighted = weight_part * flux_part
        self_term = jnp.sum(weighted * flux_part, axis=0)
        cross = jnp.einsum('bp,bk->pk', weighted, bank, precision=lax.Precision.HIGHEST)
        norm_tt = jnp.einsum('bp,bk->pk', weight_part, squared, precision=lax.Precision.HIGHEST)
        loglike = -0.5 * (self_term[:, None] - cross * cross / norm_tt)
        peak = jnp.max(loglike, axis=1)
        expo = jnp.exp(loglike - peak[:, None])
        total = jnp.sum(expo, axis=1)
        moments = jnp.einsum('pk,qk->qp', expo, coords, precision=lax.Precision.HIGHEST)
        return peak, total, moments

    peak, total, moments = lax.map(one_block, (flux_blocks, weight_blocks))
    return peak.reshape(pixels), total.reshape(pixels), moments.transpose(1, 0, 2).reshape(3, pixels)


def reference(sky_image, inverse_var, kernel_taps, kernel_sizes, templates, grid_index):
    kernel = kernel_table(kernel_taps, kernel_sizes)
    bands, height, width = sky_image.shape
    padded = jnp.pad(sky_image, ((0, 0), (RADIUS, RADIUS), (0, 0)))
    smooth = convolve_rows(padded, kernel, height)
    flux = convolve_cols(jnp.pad(smooth, ((0, 0), (0, 0), (RADIUS, RADIUS))), kernel, width)
    coords = (grid_index.astype(jnp.float32) + 0.5) / GRID
    peak, total, moments = fit_pixels(flux.reshape(bands, height * width), inverse_var.reshape(bands, height * width), templates, coords)
    post_means = (moments / total[None, :]).reshape(3, height, width)
    log_evidence = (peak + jnp.log(total)).reshape(height, width)
    return post_means, log_evidence
```

```python
import functools
import math

import jax
import jax.numpy as jnp
from jax import lax
from jax.experimental import pallas as pl
from jax.experimental.pallas import tpu as pltpu
from jax.sharding import PartitionSpec as P

GRID = 64


def with_halo(x, sides, width):
    for axis, dim in sides:
        count, length = (lax.axis_size(axis), x.shape[dim])
        up = [(i, (i + 1) % count) for i in range(count - 1)]
        down = [(j, i) for i, j in up]
        last = lax.slice_in_dim(x, length - width, length, axis=dim)
        leading = lax.slice_in_dim(x, 0, width, axis=dim)
        before = lax.ppermute(last, axis, up)
        after = lax.ppermute(leading, axis, down)
        x = jnp.concatenate([before, x, after], axis=dim)
    return x


def joined_along(pieces, dim):
    pieces = jnp.moveaxis(pieces, 0, dim)
    lengths = pieces.shape
    return pieces.reshape(*lengths[:dim], lengths[dim] * lengths[dim + 1], *lengths[dim + 2 :])


def sent_to_all(x, axis):
    copies = jnp.broadcast_to(x, (lax.axis_size(axis), *x.shape))
    return lax.all_to_all(copies, axis, split_axis=0, concat_axis=0, tiled=True)


def gather_directly(x, axis, dim):
    return joined_along(sent_to_all(x, axis), dim)


def in_one_piece(arrays, axis, dim, along):
    ends, at = ([], 0)
    for a in arrays[:-1]:
        at += a.shape[along]
        ends.append(at)
    both = jnp.concatenate(arrays, axis=along)
    return tuple(jnp.split(gather_directly(both, axis, dim), ends, axis=along))


def kernel_table(kernel_taps, kernel_sizes, radius):
    offsets = jnp.arange(2 * radius + 1, dtype=jnp.int32) - radius
    inside = jnp.abs(offsets)[None, :] <= kernel_sizes[:, None]
    masked = jnp.where(inside, kernel_taps, jnp.float32(0.0))
    return masked / jnp.sum(masked, axis=1, keepdims=True)


def convolve_rows(padded, kernel, height, radius):
    result = jnp.zeros((padded.shape[0], height, padded.shape[2]), jnp.float32)
    for offset in range(2 * radius + 1):
        result = result + kernel[:, offset, None, None] * padded[:, offset : offset + height, :]
    return result


def convolve_cols(padded, kernel, width, radius):
    result = jnp.zeros((padded.shape[0], padded.shape[1], width), jnp.float32)
    for offset in range(2 * radius + 1):
        result = result + kernel[:, offset, None, None] * padded[:, :, offset : offset + width]
    return result


SCALE = math.sqrt(0.5 / math.log(2.0))
LN2 = math.log(2.0)
BF = jnp.bfloat16

def split3(x):
    a = x.astype(BF); r = x - a.astype(jnp.float32)
    b = r.astype(BF); r = r - b.astype(jnp.float32)
    return a, b, r.astype(BF)

def recip(t):
    r = pl.reciprocal(t, approx=True)
    return r * (2.0 - t * r)

def fit_kernel(flux_ref, wt_ref, bank_ref, pm_ref, le_ref, lc, lt, cs, g_ref, *, div, nexp, KC=256):
    zeros32 = jnp.zeros((32, 128), jnp.float32)
    row16 = lax.broadcasted_iota(jnp.int32, (16, 128), 0)
    for s in range(16):
        blk = bank_ref[s]
        T = jnp.where(row16 < 10, blk, 0.0)
        for dst, X in ((lc, T), (lt, T * T)):
            a, b, c = (v.astype(jnp.float32) for v in split3(X))
            st = jnp.concatenate([a, a, b, a, b, c, zeros32], axis=0)
            dst[pl.ds(s * 128, 128), :] = st.T.astype(BF)
        cc = (2.0 * blk + 1.0) * (1.0 / 128.0)
        cc = jnp.where(row16 == 13, 1.0, jnp.where((row16 >= 10) & (row16 < 13), cc, 0.0))
        cs[:, pl.ds(s * 128, 128)] = cc.astype(BF)

    def rhs(r2):
        Fc, Ft, ffs = [], [], []
        for j in range(2):
            f = flux_ref[2 * r2 + j]; w = wt_ref[2 * r2 + j]
            wf = w * f
            ffs.append(jnp.sum(wf * f, axis=0, keepdims=True))
            wf = wf * SCALE
            a, b, c = split3(wf)
            Fc.append(jnp.concatenate([a, b, a, c, b, a, jnp.zeros((32, 128), BF)], axis=0))
            a, b, c = split3(w)
            Ft.append(jnp.concatenate([a, b, a, c, b, a, jnp.zeros((32, 128), BF)], axis=0))
        return jnp.concatenate(Fc, 1), jnp.concatenate(Ft, 1), jnp.concatenate(ffs, 1)

    def block(r2, _):
        Fc, Ft, ff = rhs(r2)
        m = None
        for ch in range(2048 // KC):
            c = jnp.dot(lc[pl.ds(ch * KC, KC), :], Fc, preferred_element_type=jnp.float32)
            t = jnp.dot(lt[pl.ds(ch * KC, KC), :], Ft, preferred_element_type=jnp.float32)
            if div == "div": g = c * c / t
            elif div == "newton":
                r = pl.reciprocal(t, approx=True)
                g = (c * r) * (c * (2.0 - t * r))
            elif div == "approx": g = c * c * pl.reciprocal(t, approx=True)
            g_ref[pl.ds(ch * KC, KC), :] = g
            mm = jnp.max(g.reshape(KC // 8, 8, 256), axis=0)
            m = mm if m is None else jnp.maximum(m, mm)
        m = jnp.max(m, axis=0, keepdims=True)
        acc = jnp.zeros((16, 256), jnp.float32)
        for ch in range(2048 // KC):
            e = jnp.exp2(g_ref[pl.ds(ch * KC, KC), :] - m)
            eh = e.astype(BF)
            acc = acc + jnp.dot(cs[:, pl.ds(ch * KC, KC)], eh, preferred_element_type=jnp.float32)
            if nexp == 2:
                el = (e - eh.astype(jnp.float32)).astype(BF)
                acc = acc + jnp.dot(cs[:, pl.ds(ch * KC, KC)], el, preferred_element_type=jnp.float32)
        tot = acc[13:14]
        pm = acc[10:13] / tot
        le = m * LN2 - 0.5 * ff + jnp.log(tot)
        for j in range(2):
            sl = slice(j * 128, j * 128 + 128)
            for q in range(3):
                pm_ref[q, pl.ds(2 * r2 + j, 1), :] = pm[q:q + 1, sl]
            le_ref[pl.ds(2 * r2 + j, 1), :] = le[:, sl]
        return 0
    lax.fori_loop(0, 8, block, 0)

def fit(flux, wt, bank, div="div", nexp=1, KC=256):
    vm = pl.BlockSpec(memory_space=pltpu.VMEM)
    return pl.pallas_call(
        functools.partial(fit_kernel, div=div, nexp=nexp, KC=KC),
        out_shape=(jax.ShapeDtypeStruct((3, 16, 128), jnp.float32), jax.ShapeDtypeStruct((16, 128), jnp.float32)),
        in_specs=[vm, vm, vm], out_specs=(vm, vm),
        scratch_shapes=[pltpu.VMEM((2048, 128), BF), pltpu.VMEM((2048, 128), BF), pltpu.VMEM((16, 2048), BF), pltpu.VMEM((2048, 256), jnp.float32)],
    )(flux, wt, bank)


def body(sky_image, inverse_var, kernel_taps, kernel_sizes, templates, grid_index):
    radius = (kernel_taps.shape[1] - 1) // 2
    bands, height, width = sky_image.shape
    shards = lax.axis_size("tmpl")
    col_block = width // shards
    col_start = lax.axis_index("tmpl") * col_block
    kernel = kernel_table(kernel_taps, kernel_sizes, radius)
    padded_cols = jnp.pad(sky_image, ((0, 0), (0, 0), (radius, radius)))
    own_cols = lax.dynamic_slice_in_dim(padded_cols, col_start, col_block + 2 * radius, 2)
    extended = with_halo(own_cols, (("tile", 1),), radius)
    smooth = convolve_rows(extended, kernel, height, radius)
    flux = convolve_cols(smooth, kernel, col_block, radius)
    own_weight = lax.dynamic_slice_in_dim(inverse_var, col_start, col_block, 2)
    bank = jnp.concatenate([templates, grid_index.astype(jnp.float32), jnp.zeros((3, templates.shape[1]), jnp.float32)], axis=0)
    bank = sent_to_all(bank, "tmpl")
    pad = ((0, 0), (0, 6), (0, 0))
    return fit(jnp.pad(flux.transpose(1, 0, 2), pad), jnp.pad(own_weight.transpose(1, 0, 2), pad), bank)


def solution(mesh):
    placed = (
        P(None, "tile", None),
        P(None, "tile", None),
        P(),
        P(),
        P(None, "tmpl"),
        P(None, "tmpl"),
    )
    return jax.shard_map(
        body,
        mesh=mesh,
        in_specs=placed,
        out_specs=(P(None, "tile", "tmpl"), P("tile", "tmpl")),
        check_vma=False,
    )
```

```python
import functools
import math

import jax
import jax.numpy as jnp
from jax import lax
from jax.experimental import pallas as pl
from jax.experimental.pallas import tpu as pltpu
from jax.sharding import PartitionSpec as P

BANDS = 10
RADIUS = 8
TAPS = 2 * RADIUS + 1
LANES = 128
SUB = 16
SCALE = math.sqrt(0.5 / math.log(2.0))
LN2 = math.log(2.0)
BF = jnp.bfloat16
F32 = jnp.float32


def prep_kernel(sky, ivar, taps, sizes, templates, grid_index, bank, first, last, weight, cols, tm, gi, tp, sz, sems):
    c = lax.axis_index("tmpl")
    shards = bank.shape[0]
    at = lambda i: pl.ds(pl.multiple_of(i * LANES, LANES), LANES)
    copies = [
        pltpu.make_async_copy(sky.at[:, :, at(jnp.maximum(c - 1, 0))], cols.at[0], sems.at[0]),
        pltpu.make_async_copy(sky.at[:, :, at(c)], cols.at[1], sems.at[1]),
        pltpu.make_async_copy(sky.at[:, :, at(jnp.minimum(c + 1, shards - 1))], cols.at[2], sems.at[2]),
        pltpu.make_async_copy(taps, tp, sems.at[3]),
        pltpu.make_async_copy(sizes, sz, sems.at[4]),
        pltpu.make_async_copy(templates, tm, sems.at[5]),
        pltpu.make_async_copy(grid_index, gi, sems.at[6]),
        pltpu.make_async_copy(ivar.at[:, :, at(c)], weight, sems.at[7]),
    ]
    for copy in copies:
        copy.start()
    copies[5].wait()
    copies[6].wait()
    rows = jnp.concatenate([tm[...], gi[...].astype(F32), jnp.zeros((SUB - BANDS - 3, LANES), F32)], axis=0)
    for s in range(shards):
        bank[s] = rows
    for copy in copies[:5]:
        copy.wait()
    lane = lax.broadcasted_iota(jnp.int32, (16, LANES), 1)
    right_ok = jnp.where(c < shards - 1, 1.0, 0.0)
    left_ok = jnp.where(c > 0, 1.0, 0.0)
    for b in range(BANDS):
        main = cols[1, b]
        side = jnp.where(lane < LANES // 2, cols[2, b] * right_ok, cols[0, b] * left_ok)
        size = sz[b]
        acc = main * tp[b, RADIUS]
        for d in range(1, RADIUS + 1):
            up = pltpu.roll(jnp.where(lane >= d, main, side), LANES - d, 1)
            down = pltpu.roll(jnp.where(lane < LANES - d, main, side), d, 1)
            acc = acc + up * jnp.where(d <= size, tp[b, RADIUS + d], 0.0)
            acc = acc + down * jnp.where(d <= size, tp[b, RADIUS - d], 0.0)
        first[pl.ds(b, 8, stride=BANDS), :] = acc[:8]
        last[pl.ds(b, 8, stride=BANDS), :] = acc[8:]
    copies[7].wait()


def prep(sky, ivar, taps, sizes, templates, grid_index, shards):
    hbm = pl.BlockSpec(memory_space=pl.ANY)
    vm = pl.BlockSpec(memory_space=pltpu.VMEM)
    halo = pltpu.VMEM((8 * BANDS, LANES), F32)
    return pl.pallas_call(
        prep_kernel,
        out_shape=(pltpu.VMEM((shards, SUB, LANES), F32), halo, halo, pltpu.VMEM((BANDS, 16, LANES), F32)),
        in_specs=[hbm] * 6,
        out_specs=(vm,) * 4,
        scratch_shapes=[
            pltpu.VMEM((3, BANDS, 16, LANES), F32),
            pltpu.VMEM((BANDS, LANES), F32),
            pltpu.VMEM((3, LANES), jnp.int32),
            pltpu.SMEM((BANDS, TAPS), F32),
            pltpu.SMEM((BANDS,), jnp.int32),
            pltpu.SemaphoreType.DMA((8,)),
        ],
        name="prep",
    )(sky, ivar, taps, sizes, templates, grid_index)


def split3(x):
    a = x.astype(BF)
    r = x - a.astype(F32)
    b = r.astype(BF)
    r = r - b.astype(F32)
    return a, b, r.astype(BF)


def fit_kernel(up, first, last, down, wt, taps, sizes, bank, pm_ref, le_ref, ext, flux, tk, lc, lt, cs, g_ref, e_ref, *, KC):
    row16 = lax.broadcasted_iota(jnp.int32, (SUB, LANES), 0)
    lane16 = lax.broadcasted_iota(jnp.int32, (SUB, LANES), 1)

    pad6 = jnp.zeros((SUB - BANDS, LANES), F32)
    for q, part in enumerate((up, first, last, down)):
        for r in range(8):
            ext[q * 8 + r] = jnp.concatenate([part[pl.ds(r * BANDS, BANDS), :], pad6], axis=0)
    tk[...] = jnp.zeros((SUB, LANES), F32)
    tk[0:BANDS, 0:TAPS] = taps[...]
    sv = jnp.zeros((SUB, LANES), jnp.int32)
    for b in range(BANDS):
        sv = jnp.where(row16 == b, sizes[b], sv)
    kern = jnp.where((jnp.abs(lane16 - RADIUS) <= sv) & (lane16 < TAPS) & (row16 < BANDS), tk[...], 0.0)
    norm = jnp.sum(kern, axis=1, keepdims=True)
    norm = jnp.where(row16 < BANDS, jnp.broadcast_to(norm, (SUB, LANES)), 1.0)
    kern = kern / (norm * norm)
    kv = [jnp.broadcast_to(kern[:, t : t + 1], (SUB, LANES)) for t in range(TAPS)]
    for r in range(16):
        acc = kv[0] * ext[r]
        for t in range(1, TAPS):
            acc = acc + kv[t] * ext[r + t]
        flux[r] = acc

    def lhs_prep(s):
        zeros32 = jnp.zeros((32, LANES), F32)
        blk = bank[s]
        T = jnp.where(row16 < BANDS, blk, 0.0)
        for dst, X in ((lc, T), (lt, T * T)):
            a, b, c = (v.astype(F32) for v in split3(X))
            st = jnp.concatenate([a, a, b, a, b, c, zeros32], axis=0)
            dst[pl.ds(s * LANES, LANES), :] = st.T.astype(BF)
        cc = (2.0 * blk + 1.0) * (1.0 / 128.0)
        cc = jnp.where(row16 == 13, 1.0, jnp.where((row16 >= 10) & (row16 < 13), cc, 0.0))
        cs[:, pl.ds(s * LANES, LANES)] = cc.astype(BF)

    def rhs(r2):
        Fc, Ft, ffs = [], [], []
        for j in range(2):
            f = flux[2 * r2 + j]
            w = jnp.concatenate([wt[pl.ds(2 * r2 + j, BANDS, stride=16), :], pad6], axis=0)
            wf = w * f
            ffs.append(jnp.sum(wf * f, axis=0, keepdims=True))
            z = jnp.zeros((32, LANES), BF)
            a, b, c = split3(wf * SCALE)
            Fc.append(jnp.concatenate([a, b, a, c, b, a, z], axis=0))
            a, b, c = split3(w)
            Ft.append(jnp.concatenate([a, b, a, c, b, a, z], axis=0))
        return jnp.concatenate(Fc, 1), jnp.concatenate(Ft, 1), jnp.concatenate(ffs, 1)

    NT = lc.shape[0]
    n1 = NT // KC

    def phase1(ch, Fc, Ft, m):
        c = jnp.dot(lc[pl.ds(ch * KC, KC), :], Fc, preferred_element_type=F32)
        t = jnp.dot(lt[pl.ds(ch * KC, KC), :], Ft, preferred_element_type=F32)
        g = c * c / t
        g_ref[pl.ds(ch * KC, KC), :] = g
        mm = jnp.max(g.reshape(KC // 8, 8, 256), axis=0)
        return mm if m is None else jnp.maximum(m, mm)

    def exps(k, m):
        e_ref[pl.ds(k * KC, KC), :] = jnp.exp2(g_ref[pl.ds(k * KC, KC), :] - m).astype(BF)

    def edot(k, acc):
        d = jnp.dot(cs[:, pl.ds(k * KC, KC)], e_ref[pl.ds(k * KC, KC), :], preferred_element_type=F32)
        return d if acc is None else acc + d

    def finish(r2, m, ff, acc):
        tot = acc[13:14]
        pm = acc[10:13] / tot
        le = m * LN2 - 0.5 * ff + jnp.log(tot)
        for j in range(2):
            sl = slice(j * LANES, j * LANES + LANES)
            for q in range(3):
                pm_ref[q, pl.ds(2 * r2 + j, 1), :] = pm[q : q + 1, sl]
            le_ref[pl.ds(2 * r2 + j, 1), :] = le[:, sl]

    Fc, Ft, ff0 = rhs(0)
    m = None
    for ch in range(n1):
        for s in range(ch * KC // LANES, (ch + 1) * KC // LANES):
            lhs_prep(s)
        m = phase1(ch, Fc, Ft, m)
    m0 = jnp.max(m, axis=0, keepdims=True)

    def body(i, carry):
        mp, ffp = carry
        Fc, Ft, ff = rhs(i)
        m = acc = None
        for ch in range(n1):
            if ch >= 1:
                acc = edot(ch - 1, acc)
            exps(ch, mp)
            m = phase1(ch, Fc, Ft, m)
        acc = edot(n1 - 1, acc)
        finish(i - 1, mp, ffp, acc)
        return jnp.max(m, axis=0, keepdims=True), ff

    mp, ffp = lax.fori_loop(1, 8, body, (m0, ff0))
    acc = None
    for k in range(n1):
        exps(k, mp)
        acc = edot(k, acc)
    finish(7, mp, ffp, acc)


def fit(up, first, last, down, wt, taps, sizes, bank, KC=256):
    vm = pl.BlockSpec(memory_space=pltpu.VMEM)
    sm = pl.BlockSpec(memory_space=pltpu.SMEM)
    nt = bank.shape[0] * LANES
    on_chip = lambda x: pltpu.with_memory_space_constraint(x, pltpu.VMEM)
    return pl.pallas_call(
        functools.partial(fit_kernel, KC=KC),
        out_shape=(jax.ShapeDtypeStruct((3, 16, LANES), F32), jax.ShapeDtypeStruct((16, LANES), F32)),
        in_specs=[vm, vm, vm, vm, vm, vm, sm, vm],
        out_specs=(vm, vm),
        scratch_shapes=[
            pltpu.VMEM((32, SUB, LANES), F32),
            pltpu.VMEM((16, SUB, LANES), F32),
            pltpu.VMEM((SUB, LANES), F32),
            pltpu.VMEM((nt, LANES), BF),
            pltpu.VMEM((nt, LANES), BF),
            pltpu.VMEM((SUB, nt), BF),
            pltpu.VMEM((nt, 256), F32),
            pltpu.VMEM((nt, 256), BF),
        ],
        name="fit",
    )(on_chip(up), on_chip(first), on_chip(last), on_chip(down), on_chip(wt.reshape(BANDS * 16, LANES)), taps, sizes, on_chip(bank))


def body(sky_image, inverse_var, kernel_taps, kernel_sizes, templates, grid_index):
    shards = lax.axis_size("tmpl")
    tiles = lax.axis_size("tile")
    bank, first, last, weight = prep(sky_image, inverse_var, kernel_taps, kernel_sizes, templates, grid_index, shards)
    bank = lax.all_to_all(bank, "tmpl", split_axis=0, concat_axis=0, tiled=True)
    ups = [(i, i + 1) for i in range(tiles - 1)]
    before = lax.ppermute(last, "tile", ups)
    after = lax.ppermute(first, "tile", [(j, i) for i, j in ups])
    return fit(before, first, last, after, weight, kernel_taps, kernel_sizes, bank)


def solution(mesh):
    placed = (
        P(None, "tile", None),
        P(None, "tile", None),
        P(),
        P(),
        P(None, "tmpl"),
        P(None, "tmpl"),
    )
    return jax.shard_map(
        body,
        mesh=mesh,
        in_specs=placed,
        out_specs=(P(None, "tile", "tmpl"), P("tile", "tmpl")),
        check_vma=False,
    )
```

```python
import functools
import math

import jax
import jax.numpy as jnp
from jax import lax
from jax.experimental import pallas as pl
from jax.experimental.pallas import tpu as pltpu
from jax.sharding import PartitionSpec as P

BANDS = 10
RADIUS = 8
TAPS = 2 * RADIUS + 1
LANES = 128
SUB = 16
SCALE = math.sqrt(0.5 / math.log(2.0))
LN2 = math.log(2.0)
BF = jnp.bfloat16
F32 = jnp.float32


def bank_kernel(templates, grid_index, bank, rows, gi, sems):
    shards = bank.shape[0]
    reads = [
        pltpu.make_async_copy(templates, rows.at[0:BANDS], sems.at[0]),
        pltpu.make_async_copy(grid_index, gi, sems.at[1]),
    ]
    for copy in reads:
        copy.start()
    for copy in reads:
        copy.wait()
    rows[BANDS : BANDS + 3] = gi[...].astype(F32)
    rows[BANDS + 3 : SUB] = jnp.zeros((SUB - BANDS - 3, LANES), F32)
    writes = [pltpu.make_async_copy(rows, bank.at[s], sems.at[2 + s]) for s in range(shards)]
    for copy in writes:
        copy.start()
    for copy in writes:
        copy.wait()


def bank_copies(templates, grid_index, shards):
    hbm = pl.BlockSpec(memory_space=pl.ANY)
    return pl.pallas_call(
        bank_kernel,
        out_shape=jax.ShapeDtypeStruct((shards, SUB, LANES), F32),
        in_specs=[hbm] * 2,
        out_specs=hbm,
        scratch_shapes=[
            pltpu.VMEM((SUB, LANES), F32),
            pltpu.VMEM((3, LANES), jnp.int32),
            pltpu.SemaphoreType.DMA((2 + shards,)),
        ],
        name="bank",
    )(templates, grid_index)


def prep_kernel(sky, ivar, taps, sizes, far, near, weight, cols, tp, sz, sems, *, shards):
    c = lax.axis_index("tmpl")
    odd = lax.rem(lax.axis_index("tile"), 2) == 1
    at = lambda i: pl.ds(pl.multiple_of(i * LANES, LANES), LANES)
    copies = [
        pltpu.make_async_copy(sky.at[:, :, at(jnp.maximum(c - 1, 0))], cols.at[0], sems.at[0]),
        pltpu.make_async_copy(sky.at[:, :, at(c)], cols.at[1], sems.at[1]),
        pltpu.make_async_copy(sky.at[:, :, at(jnp.minimum(c + 1, shards - 1))], cols.at[2], sems.at[2]),
        pltpu.make_async_copy(taps, tp, sems.at[3]),
        pltpu.make_async_copy(sizes, sz, sems.at[4]),
        pltpu.make_async_copy(ivar.at[:, :, at(c)], weight, sems.at[5]),
    ]
    for copy in copies:
        copy.start()
    for copy in copies[:5]:
        copy.wait()
    lane = lax.broadcasted_iota(jnp.int32, (16, LANES), 1)
    right_ok = jnp.where(c < shards - 1, 1.0, 0.0)
    left_ok = jnp.where(c > 0, 1.0, 0.0)
    for b in range(BANDS):
        main = cols[1, b]
        side = jnp.where(lane < LANES // 2, cols[2, b] * right_ok, cols[0, b] * left_ok)
        size = sz[b]
        acc = main * tp[b, RADIUS]
        for d in range(1, RADIUS + 1):
            up = pltpu.roll(jnp.where(lane >= d, main, side), LANES - d, 1)
            down = pltpu.roll(jnp.where(lane < LANES - d, main, side), d, 1)
            acc = acc + up * jnp.where(d <= size, tp[b, RADIUS + d], 0.0)
            acc = acc + down * jnp.where(d <= size, tp[b, RADIUS - d], 0.0)
        near[pl.ds(b, 8, stride=BANDS), :] = jnp.where(odd, acc[:8], acc[8:])
        far[pl.ds(b, 8, stride=BANDS), :] = jnp.where(odd, acc[8:], acc[:8])
    copies[5].wait()


def prep(sky, ivar, taps, sizes, shards):
    hbm = pl.BlockSpec(memory_space=pl.ANY)
    vm = pl.BlockSpec(memory_space=pltpu.VMEM)
    halo = pltpu.VMEM((8 * BANDS, LANES), F32)
    return pl.pallas_call(
        functools.partial(prep_kernel, shards=shards),
        out_shape=(halo, halo, pltpu.VMEM((BANDS, 16, LANES), F32)),
        in_specs=[hbm] * 4,
        out_specs=(vm,) * 3,
        scratch_shapes=[
            pltpu.VMEM((3, BANDS, 16, LANES), F32),
            pltpu.SMEM((BANDS, TAPS), F32),
            pltpu.SMEM((BANDS,), jnp.int32),
            pltpu.SemaphoreType.DMA((6,)),
        ],
        name="prep",
    )(sky, ivar, taps, sizes)


def split3(x):
    a = x.astype(BF)
    r = x - a.astype(F32)
    b = r.astype(BF)
    r = r - b.astype(F32)
    return a, b, r.astype(BF)


def rows_kernel(got_far, got_near, far, near, wt, taps, sizes, fc_ref, ft_ref, ff_ref, ext, tk):
    row16 = lax.broadcasted_iota(jnp.int32, (SUB, LANES), 0)
    lane16 = lax.broadcasted_iota(jnp.int32, (SUB, LANES), 1)
    odd = lax.rem(lax.axis_index("tile"), 2)
    pad6 = jnp.zeros((SUB - BANDS, LANES), F32)
    for base, part in ((24 - 24 * odd, got_near), (24 * odd, got_far), (16 - 8 * odd, near), (8 + 8 * odd, far)):
        for r in range(8):
            ext[base + r] = jnp.concatenate([part[pl.ds(r * BANDS, BANDS), :], pad6], axis=0)
    tk[...] = jnp.zeros((SUB, LANES), F32)
    tk[0:BANDS, 0:TAPS] = taps[...]
    sv = jnp.zeros((SUB, LANES), jnp.int32)
    for b in range(BANDS):
        sv = jnp.where(row16 == b, sizes[b], sv)
    kern = jnp.where((jnp.abs(lane16 - RADIUS) <= sv) & (lane16 < TAPS) & (row16 < BANDS), tk[...], 0.0)
    norm = jnp.sum(kern, axis=1, keepdims=True)
    norm = jnp.where(row16 < BANDS, jnp.broadcast_to(norm, (SUB, LANES)), 1.0)
    kern = kern / (norm * norm)
    kv = [jnp.broadcast_to(kern[:, t : t + 1], (SUB, LANES)) for t in range(TAPS)]
    z = jnp.zeros((32, LANES), BF)
    for r in range(16):
        f = kv[0] * ext[r]
        for t in range(1, TAPS):
            f = f + kv[t] * ext[r + t]
        w = jnp.concatenate([wt[pl.ds(r, BANDS, stride=16), :], pad6], axis=0)
        wf = w * f
        ff_ref[pl.ds(r, 1), :] = jnp.sum(wf * f, axis=0, keepdims=True)
        at = pl.ds((r % 2) * LANES, LANES)
        for ref, x in ((fc_ref, wf * SCALE), (ft_ref, w)):
            a, b, c = split3(x)
            ref[r // 2, :, at] = jnp.concatenate([a, b, a, c, b, a, z], axis=0)


def rows(got_far, got_near, far, near, wt, taps, sizes):
    vm = pl.BlockSpec(memory_space=pltpu.VMEM)
    sm = pl.BlockSpec(memory_space=pltpu.SMEM)
    on_chip = lambda x: pltpu.with_memory_space_constraint(x, pltpu.VMEM)
    side = pltpu.VMEM((8, LANES, 2 * LANES), BF)
    return pl.pallas_call(
        rows_kernel,
        out_shape=(side, side, pltpu.VMEM((16, LANES), F32)),
        in_specs=[vm, vm, vm, vm, vm, vm, sm],
        out_specs=(vm, vm, vm),
        scratch_shapes=[pltpu.VMEM((32, SUB, LANES), F32), pltpu.VMEM((SUB, LANES), F32)],
        name="rows",
    )(on_chip(got_far), on_chip(got_near), on_chip(far), on_chip(near), on_chip(wt.reshape(BANDS * 16, LANES)), taps, sizes)


def fit_kernel(fc_ref, ft_ref, ff_ref, bank, pm_ref, le_ref, lc, lt, cs, g_ref, e_ref, *, KC):
    row16 = lax.broadcasted_iota(jnp.int32, (SUB, LANES), 0)

    def lhs_prep(s):
        zeros32 = jnp.zeros((32, LANES), F32)
        blk = bank[s]
        T = jnp.where(row16 < BANDS, blk, 0.0)
        for dst, X in ((lc, T), (lt, T * T)):
            a, b, c = (v.astype(F32) for v in split3(X))
            st = jnp.concatenate([a, a, b, a, b, c, zeros32], axis=0)
            dst[pl.ds(s * LANES, LANES), :] = st.T.astype(BF)
        cc = (2.0 * blk + 1.0) * (1.0 / 128.0)
        cc = jnp.where(row16 == 13, 1.0, jnp.where((row16 >= 10) & (row16 < 13), cc, 0.0))
        cs[:, pl.ds(s * LANES, LANES)] = cc.astype(BF)

    NT = lc.shape[0]
    n1 = NT // KC

    def phase1(ch, Fc, Ft, m):
        c = jnp.dot(lc[pl.ds(ch * KC, KC), :], Fc, preferred_element_type=F32)
        t = jnp.dot(lt[pl.ds(ch * KC, KC), :], Ft, preferred_element_type=F32)
        g = c * c / t
        g_ref[pl.ds(ch * KC, KC), :] = g
        mm = jnp.max(g.reshape(KC // 8, 8, 256), axis=0)
        return mm if m is None else jnp.maximum(m, mm)

    def exps(k, m):
        e_ref[pl.ds(k * KC, KC), :] = jnp.exp2(g_ref[pl.ds(k * KC, KC), :] - m).astype(BF)

    def edot(k, acc):
        d = jnp.dot(cs[:, pl.ds(k * KC, KC)], e_ref[pl.ds(k * KC, KC), :], preferred_element_type=F32)
        return d if acc is None else acc + d

    def finish(r2, m, acc):
        tot = acc[13:14]
        pm = acc[10:13] / tot
        le = m * LN2 + jnp.log(tot)
        for j in range(2):
            sl = slice(j * LANES, j * LANES + LANES)
            for q in range(3):
                pm_ref[q, pl.ds(2 * r2 + j, 1), :] = pm[q : q + 1, sl]
            at = pl.ds(2 * r2 + j, 1)
            le_ref[at, :] = le[:, sl] - 0.5 * ff_ref[at, :]

    Fc, Ft = fc_ref[0], ft_ref[0]
    m = None
    for ch in range(n1):
        for s in range(ch * KC // LANES, (ch + 1) * KC // LANES):
            lhs_prep(s)
        m = phase1(ch, Fc, Ft, m)
    m0 = jnp.max(m, axis=0, keepdims=True)

    def body(i, mp):
        Fc, Ft = fc_ref[i], ft_ref[i]
        m = acc = None
        for ch in range(n1):
            if ch >= 1:
                acc = edot(ch - 1, acc)
            exps(ch, mp)
            m = phase1(ch, Fc, Ft, m)
        acc = edot(n1 - 1, acc)
        finish(i - 1, mp, acc)
        return jnp.max(m, axis=0, keepdims=True)

    mp = lax.fori_loop(1, 8, body, m0)
    acc = None
    for k in range(n1):
        exps(k, mp)
        acc = edot(k, acc)
    finish(7, mp, acc)


def fit(fc, ft, ff, bank, KC=256):
    vm = pl.BlockSpec(memory_space=pltpu.VMEM)
    nt = bank.shape[0] * LANES
    on_chip = lambda x: pltpu.with_memory_space_constraint(x, pltpu.VMEM)
    return pl.pallas_call(
        functools.partial(fit_kernel, KC=KC),
        out_shape=(jax.ShapeDtypeStruct((3, 16, LANES), F32), jax.ShapeDtypeStruct((16, LANES), F32)),
        in_specs=[vm] * 4,
        out_specs=(vm, vm),
        scratch_shapes=[
            pltpu.VMEM((nt, LANES), BF),
            pltpu.VMEM((nt, LANES), BF),
            pltpu.VMEM((SUB, nt), BF),
            pltpu.VMEM((nt, 256), F32),
            pltpu.VMEM((nt, 256), BF),
        ],
        name="fit",
    )(on_chip(fc), on_chip(ft), on_chip(ff), on_chip(bank))


def swaps(start, count):
    pairs = [(i, i + 1) for i in range(start, count - 1, 2)]
    return pairs + [(j, i) for i, j in pairs]


def body(sky_image, inverse_var, kernel_taps, kernel_sizes, templates, grid_index):
    shards = lax.axis_size("tmpl")
    tiles = lax.axis_size("tile")
    bank = bank_copies(templates, grid_index, shards)
    bank = lax.all_to_all(bank, "tmpl", split_axis=0, concat_axis=0, tiled=True)
    far, near, weight = prep(sky_image, inverse_var, kernel_taps, kernel_sizes, shards)
    got_far = lax.ppermute(far, "tile", swaps(1, tiles))
    got_near = lax.ppermute(near, "tile", swaps(0, tiles))
    fc, ft, ff = rows(got_far, got_near, far, near, weight, kernel_taps, kernel_sizes)
    return fit(fc, ft, ff, bank)


def solution(mesh):
    placed = (
        P(None, "tile", None),
        P(None, "tile", None),
        P(),
        P(),
        P(None, "tmpl"),
        P(None, "tmpl"),
    )
    return jax.shard_map(
        body,
        mesh=mesh,
        in_specs=placed,
        out_specs=(P(None, "tile", "tmpl"), P("tile", "tmpl")),
        check_vma=False,
    )
```

```python
import functools
import math

import jax
import jax.numpy as jnp
from jax import lax
from jax.experimental import pallas as pl
from jax.experimental.pallas import tpu as pltpu
from jax.sharding import PartitionSpec as P

BANDS = 10
RADIUS = 8
TAPS = 2 * RADIUS + 1
LANES = 128
SUB = 16
SCALE = math.sqrt(0.5 / math.log(2.0))
LN2 = math.log(2.0)
BF = jnp.bfloat16
F32 = jnp.float32


def head_kernel(
    sky, ivar, taps, sizes, templates, grid_index, bank, cols, weight, kv, rows, gi, tk, sz, sems, bank_sems
):
    c = lax.axis_index("tmpl")
    shards = bank.shape[0]
    at = lambda i: pl.ds(pl.multiple_of(i * LANES, LANES), LANES)
    reads = [
        pltpu.make_async_copy(templates, rows.at[0:BANDS], sems.at[0]),
        pltpu.make_async_copy(grid_index, gi, sems.at[1]),
        pltpu.make_async_copy(taps, tk, sems.at[2]),
        pltpu.make_async_copy(sizes, sz, sems.at[3]),
        pltpu.make_async_copy(sky.at[:, :, at(jnp.maximum(c - 1, 0))], cols.at[0], sems.at[4]),
        pltpu.make_async_copy(sky.at[:, :, at(c)], cols.at[1], sems.at[5]),
        pltpu.make_async_copy(sky.at[:, :, at(jnp.minimum(c + 1, shards - 1))], cols.at[2], sems.at[6]),
        pltpu.make_async_copy(ivar.at[:, :, at(c)], weight, sems.at[7]),
    ]
    for copy in reads:
        copy.start()
    rows[BANDS + 3 : SUB] = jnp.zeros((SUB - BANDS - 3, LANES), F32)
    reads[1].wait()
    rows[BANDS : BANDS + 3] = gi[...].astype(F32)
    reads[0].wait()
    writes = [pltpu.make_async_copy(rows, bank.at[s], bank_sems.at[s]) for s in range(shards)]
    for copy in writes:
        copy.start()
    reads[2].wait()
    reads[3].wait()
    band = lax.broadcasted_iota(jnp.int32, (BANDS, TAPS), 0)
    tap = lax.broadcasted_iota(jnp.int32, (BANDS, TAPS), 1)
    half = jnp.zeros((BANDS, TAPS), jnp.int32)
    for b in range(BANDS):
        half = jnp.where(band == b, sz[b], half)
    kern = jnp.where(jnp.abs(tap - RADIUS) <= half, tk[...], 0.0)
    kern = kern / jnp.sum(kern, axis=1, keepdims=True)
    for t in range(TAPS):
        kv[t, 0:BANDS] = jnp.broadcast_to(kern[:, t : t + 1], (BANDS, LANES))
        kv[t, BANDS:SUB] = jnp.zeros((SUB - BANDS, LANES), F32)
    for copy in reads[4:]:
        copy.wait()
    for copy in writes:
        copy.wait()


def head(sky, ivar, taps, sizes, templates, grid_index, shards):
    hbm = pl.BlockSpec(memory_space=pl.ANY)
    vm = pl.BlockSpec(memory_space=pltpu.VMEM)
    return pl.pallas_call(
        head_kernel,
        out_shape=(
            jax.ShapeDtypeStruct((shards, SUB, LANES), F32),
            pltpu.VMEM((3, BANDS, 16, LANES), F32),
            pltpu.VMEM((BANDS, 16, LANES), F32),
            pltpu.VMEM((TAPS, SUB, LANES), F32),
        ),
        in_specs=[hbm] * 6,
        out_specs=(hbm, vm, vm, vm),
        scratch_shapes=[
            pltpu.VMEM((SUB, LANES), F32),
            pltpu.VMEM((3, LANES), jnp.int32),
            pltpu.VMEM((BANDS, TAPS), F32),
            pltpu.SMEM((BANDS,), jnp.int32),
            pltpu.SemaphoreType.DMA((8,)),
            pltpu.SemaphoreType.DMA((shards,)),
        ],
        name="head",
    )(sky, ivar, taps, sizes, templates, grid_index)


def columns_kernel(cols, kv, far, near, *, shards):
    c = lax.axis_index("tmpl")
    odd = lax.rem(lax.axis_index("tile"), 2) == 1
    lane = lax.broadcasted_iota(jnp.int32, (16, LANES), 1)
    right_ok = jnp.where(c < shards - 1, 1.0, 0.0)
    left_ok = jnp.where(c > 0, 1.0, 0.0)
    for b in range(BANDS):
        main = cols[1, b]
        side = jnp.where(lane < LANES // 2, cols[2, b] * right_ok, cols[0, b] * left_ok)
        tap = lambda t: jnp.broadcast_to(kv[t, b : b + 1, :], (16, LANES))
        acc = main * tap(RADIUS)
        for d in range(1, RADIUS + 1):
            up = pltpu.roll(jnp.where(lane >= d, main, side), LANES - d, 1)
            down = pltpu.roll(jnp.where(lane < LANES - d, main, side), d, 1)
            acc = acc + up * tap(RADIUS + d)
            acc = acc + down * tap(RADIUS - d)
        far[pl.ds(b, 8, stride=BANDS), :] = jnp.where(odd, acc[8:], acc[:8])
        near[pl.ds(b, 8, stride=BANDS), :] = jnp.where(odd, acc[:8], acc[8:])


def on_chip(x):
    return pltpu.with_memory_space_constraint(x, pltpu.VMEM)


def columns(cols, kv, shards):
    vm = pl.BlockSpec(memory_space=pltpu.VMEM)
    part = pltpu.VMEM((8 * BANDS, LANES), F32)
    return pl.pallas_call(
        functools.partial(columns_kernel, shards=shards),
        out_shape=(part, part),
        in_specs=[vm] * 2,
        out_specs=(vm,) * 2,
        name="columns",
    )(on_chip(cols), on_chip(kv))


def split3(x):
    a = x.astype(BF)
    r = x - a.astype(F32)
    b = r.astype(BF)
    r = r - b.astype(F32)
    return a, b, r.astype(BF)


def rows_kernel(got_far, got_near, far, near, wt, kv, fc_ref, ft_ref, ff_ref, ext):
    odd = lax.rem(lax.axis_index("tile"), 2)
    pad6 = jnp.zeros((SUB - BANDS, LANES), F32)
    for base, part in ((24 - 24 * odd, got_near), (24 * odd, got_far), (16 - 8 * odd, near), (8 + 8 * odd, far)):
        for r in range(8):
            ext[base + r] = jnp.concatenate([part[pl.ds(r * BANDS, BANDS), :], pad6], axis=0)
    z = jnp.zeros((32, LANES), BF)
    for r in range(16):
        f = kv[0] * ext[r]
        for t in range(1, TAPS):
            f = f + kv[t] * ext[r + t]
        w = jnp.concatenate([wt[pl.ds(r, BANDS, stride=16), :], pad6], axis=0)
        wf = w * f
        ff_ref[pl.ds(r, 1), :] = jnp.sum(wf * f, axis=0, keepdims=True)
        at = pl.ds((r % 2) * LANES, LANES)
        for ref, x in ((fc_ref, wf * SCALE), (ft_ref, w)):
            a, b, c = split3(x)
            ref[r // 2, :, at] = jnp.concatenate([a, b, a, c, b, a, z], axis=0)


def rows(got_far, got_near, far, near, wt, kv):
    vm = pl.BlockSpec(memory_space=pltpu.VMEM)
    side = pltpu.VMEM((8, LANES, 2 * LANES), BF)
    return pl.pallas_call(
        rows_kernel,
        out_shape=(side, side, pltpu.VMEM((16, LANES), F32)),
        in_specs=[vm] * 6,
        out_specs=(vm,) * 3,
        scratch_shapes=[pltpu.VMEM((32, SUB, LANES), F32)],
        name="rows",
    )(on_chip(got_far), on_chip(got_near), on_chip(far), on_chip(near), on_chip(wt.reshape(BANDS * 16, LANES)), on_chip(kv))


def fit_kernel(fc_ref, ft_ref, ff_ref, bank, pm_ref, le_ref, lc, lt, cs, g_ref, e_ref, *, KC):
    row16 = lax.broadcasted_iota(jnp.int32, (SUB, LANES), 0)

    def lhs_prep(s):
        zeros32 = jnp.zeros((32, LANES), F32)
        blk = bank[s]
        T = jnp.where(row16 < BANDS, blk, 0.0)
        for dst, X in ((lc, T), (lt, T * T)):
            a, b, c = (v.astype(F32) for v in split3(X))
            st = jnp.concatenate([a, a, b, a, b, c, zeros32], axis=0)
            dst[pl.ds(s * LANES, LANES), :] = st.T.astype(BF)
        cc = (2.0 * blk + 1.0) * (1.0 / 128.0)
        cc = jnp.where(row16 == 13, 1.0, jnp.where((row16 >= 10) & (row16 < 13), cc, 0.0))
        cs[:, pl.ds(s * LANES, LANES)] = cc.astype(BF)

    NT = lc.shape[0]
    n1 = NT // KC

    def phase1(ch, Fc, Ft, m):
        c = jnp.dot(lc[pl.ds(ch * KC, KC), :], Fc, preferred_element_type=F32)
        t = jnp.dot(lt[pl.ds(ch * KC, KC), :], Ft, preferred_element_type=F32)
        g = c * c / t
        g_ref[pl.ds(ch * KC, KC), :] = g
        mm = jnp.max(g.reshape(KC // 8, 8, 256), axis=0)
        return mm if m is None else jnp.maximum(m, mm)

    def exps(k, m):
        e_ref[pl.ds(k * KC, KC), :] = jnp.exp2(g_ref[pl.ds(k * KC, KC), :] - m).astype(BF)

    def edot(k, acc):
        d = jnp.dot(cs[:, pl.ds(k * KC, KC)], e_ref[pl.ds(k * KC, KC), :], preferred_element_type=F32)
        return d if acc is None else acc + d

    def finish(r2, m, acc):
        tot = acc[13:14]
        pm = acc[10:13] / tot
        le = m * LN2 + jnp.log(tot)
        for j in range(2):
            sl = slice(j * LANES, j * LANES + LANES)
            for q in range(3):
                pm_ref[q, pl.ds(2 * r2 + j, 1), :] = pm[q : q + 1, sl]
            at = pl.ds(2 * r2 + j, 1)
            le_ref[at, :] = le[:, sl] - 0.5 * ff_ref[at, :]

    Fc, Ft = fc_ref[0], ft_ref[0]
    m = None
    for ch in range(n1):
        for s in range(ch * KC // LANES, (ch + 1) * KC // LANES):
            lhs_prep(s)
        m = phase1(ch, Fc, Ft, m)
    m0 = jnp.max(m, axis=0, keepdims=True)

    def body(i, mp):
        Fc, Ft = fc_ref[i], ft_ref[i]
        m = acc = None
        for ch in range(n1):
            exps(ch, mp)
            m = phase1(ch, Fc, Ft, m)
            if ch >= 1:
                acc = edot(ch - 1, acc)
        acc = edot(n1 - 1, acc)
        finish(i - 1, mp, acc)
        return jnp.max(m, axis=0, keepdims=True)

    mp = lax.fori_loop(1, 8, body, m0)
    acc = None
    for k in range(n1):
        exps(k, mp)
        acc = edot(k, acc)
    finish(7, mp, acc)


def fit(fc, ft, ff, bank, KC=256):
    vm = pl.BlockSpec(memory_space=pltpu.VMEM)
    nt = bank.shape[0] * LANES
    return pl.pallas_call(
        functools.partial(fit_kernel, KC=KC),
        out_shape=(jax.ShapeDtypeStruct((3, 16, LANES), F32), jax.ShapeDtypeStruct((16, LANES), F32)),
        in_specs=[vm] * 4,
        out_specs=(vm, vm),
        scratch_shapes=[
            pltpu.VMEM((nt, LANES), BF),
            pltpu.VMEM((nt, LANES), BF),
            pltpu.VMEM((SUB, nt), BF),
            pltpu.VMEM((nt, 256), F32),
            pltpu.VMEM((nt, 256), BF),
        ],
        name="fit",
    )(on_chip(fc), on_chip(ft), on_chip(ff), on_chip(bank))


def swaps(start, count):
    pairs = [(i, i + 1) for i in range(start, count - 1, 2)]
    return pairs + [(j, i) for i, j in pairs]


def body(sky_image, inverse_var, kernel_taps, kernel_sizes, templates, grid_index):
    shards = lax.axis_size("tmpl")
    tiles = lax.axis_size("tile")
    bank, cols, weight, kv = head(sky_image, inverse_var, kernel_taps, kernel_sizes, templates, grid_index, shards)
    bank = lax.all_to_all(bank, "tmpl", split_axis=0, concat_axis=0, tiled=True)
    far, near = columns(cols, kv, shards)
    got_far = lax.ppermute(far, "tile", swaps(1, tiles))
    got_near = lax.ppermute(near, "tile", swaps(0, tiles))
    fc, ft, ff = rows(got_far, got_near, far, near, weight, kv)
    return fit(fc, ft, ff, bank)


def solution(mesh):
    placed = (
        P(None, "tile", None),
        P(None, "tile", None),
        P(),
        P(),
        P(None, "tmpl"),
        P(None, "tmpl"),
    )
    return jax.shard_map(
        body,
        mesh=mesh,
        in_specs=placed,
        out_specs=(P(None, "tile", "tmpl"), P("tile", "tmpl")),
        check_vma=False,
    )
```

```python
import functools
import math

import jax
import jax.numpy as jnp
from jax import lax
from jax.experimental import pallas as pl
from jax.experimental.pallas import tpu as pltpu
from jax.sharding import PartitionSpec as P

BANDS = 10
RADIUS = 8
TAPS = 2 * RADIUS + 1
LANES = 128
SUB = 16
SCALE = math.sqrt(0.5 / math.log(2.0))
LN2 = math.log(2.0)
BF = jnp.bfloat16
F32 = jnp.float32


def head_kernel(
    sky, ivar, taps, sizes, templates, grid_index, bank, cols, weight, kv, rows, gi, tk, sz, sems, bank_sems
):
    c = lax.axis_index("tmpl")
    shards = bank.shape[0]
    at = lambda i: pl.ds(pl.multiple_of(i * LANES, LANES), LANES)
    reads = [
        pltpu.make_async_copy(templates, rows.at[0:BANDS], sems.at[0]),
        pltpu.make_async_copy(grid_index, gi, sems.at[1]),
        pltpu.make_async_copy(taps, tk, sems.at[2]),
        pltpu.make_async_copy(sizes, sz, sems.at[3]),
        pltpu.make_async_copy(sky.at[:, :, at(jnp.maximum(c - 1, 0))], cols.at[0], sems.at[4]),
        pltpu.make_async_copy(sky.at[:, :, at(c)], cols.at[1], sems.at[5]),
        pltpu.make_async_copy(sky.at[:, :, at(jnp.minimum(c + 1, shards - 1))], cols.at[2], sems.at[6]),
        pltpu.make_async_copy(ivar.at[:, :, at(c)], weight, sems.at[7]),
    ]
    for copy in reads:
        copy.start()
    rows[BANDS + 3 : SUB] = jnp.zeros((SUB - BANDS - 3, LANES), F32)
    reads[1].wait()
    rows[BANDS : BANDS + 3] = gi[...].astype(F32)
    reads[0].wait()
    writes = [pltpu.make_async_copy(rows, bank.at[s], bank_sems.at[s]) for s in range(shards)]
    for copy in writes:
        copy.start()
    reads[2].wait()
    reads[3].wait()
    band = lax.broadcasted_iota(jnp.int32, (BANDS, TAPS), 0)
    tap = lax.broadcasted_iota(jnp.int32, (BANDS, TAPS), 1)
    half = jnp.zeros((BANDS, TAPS), jnp.int32)
    for b in range(BANDS):
        half = jnp.where(band == b, sz[b], half)
    kern = jnp.where(jnp.abs(tap - RADIUS) <= half, tk[...], 0.0)
    kern = kern / jnp.sum(kern, axis=1, keepdims=True)
    for t in range(TAPS):
        kv[t, 0:BANDS] = jnp.broadcast_to(kern[:, t : t + 1], (BANDS, LANES))
        kv[t, BANDS:SUB] = jnp.zeros((SUB - BANDS, LANES), F32)
    for copy in reads[4:]:
        copy.wait()
    for copy in writes:
        copy.wait()


def head(sky, ivar, taps, sizes, templates, grid_index, shards):
    hbm = pl.BlockSpec(memory_space=pl.ANY)
    vm = pl.BlockSpec(memory_space=pltpu.VMEM)
    return pl.pallas_call(
        head_kernel,
        out_shape=(
            jax.ShapeDtypeStruct((shards, SUB, LANES), F32),
            pltpu.VMEM((3, BANDS, 16, LANES), F32),
            pltpu.VMEM((BANDS, 16, LANES), F32),
            pltpu.VMEM((TAPS, SUB, LANES), F32),
        ),
        in_specs=[hbm] * 6,
        out_specs=(hbm, vm, vm, vm),
        scratch_shapes=[
            pltpu.VMEM((SUB, LANES), F32),
            pltpu.VMEM((3, LANES), jnp.int32),
            pltpu.VMEM((BANDS, TAPS), F32),
            pltpu.SMEM((BANDS,), jnp.int32),
            pltpu.SemaphoreType.DMA((8,)),
            pltpu.SemaphoreType.DMA((shards,)),
        ],
        name="head",
    )(sky, ivar, taps, sizes, templates, grid_index)


def columns_kernel(cols, kv, far, near, *, shards):
    c = lax.axis_index("tmpl")
    odd = lax.rem(lax.axis_index("tile"), 2) == 1
    lane = lax.broadcasted_iota(jnp.int32, (16, LANES), 1)
    right_ok = jnp.where(c < shards - 1, 1.0, 0.0)
    left_ok = jnp.where(c > 0, 1.0, 0.0)
    for b in range(BANDS):
        main = cols[1, b]
        side = jnp.where(lane < LANES // 2, cols[2, b] * right_ok, cols[0, b] * left_ok)
        tap = lambda t: jnp.broadcast_to(kv[t, b : b + 1, :], (16, LANES))
        acc = main * tap(RADIUS)
        for d in range(1, RADIUS + 1):
            up = pltpu.roll(jnp.where(lane >= d, main, side), LANES - d, 1)
            down = pltpu.roll(jnp.where(lane < LANES - d, main, side), d, 1)
            acc = acc + up * tap(RADIUS + d)
            acc = acc + down * tap(RADIUS - d)
        far[pl.ds(b, 8, stride=BANDS), :] = jnp.where(odd, acc[8:], acc[:8])
        near[pl.ds(b, 8, stride=BANDS), :] = jnp.where(odd, acc[:8], acc[8:])


def on_chip(x):
    return pltpu.with_memory_space_constraint(x, pltpu.VMEM)


def columns(cols, kv, shards):
    vm = pl.BlockSpec(memory_space=pltpu.VMEM)
    part = pltpu.VMEM((8 * BANDS, LANES), F32)
    return pl.pallas_call(
        functools.partial(columns_kernel, shards=shards),
        out_shape=(part, part),
        in_specs=[vm] * 2,
        out_specs=(vm,) * 2,
        name="columns",
    )(on_chip(cols), on_chip(kv))


def split3(x):
    a = x.astype(BF)
    r = x - a.astype(F32)
    b = r.astype(BF)
    r = r - b.astype(F32)
    return a, b, r.astype(BF)


def rows_kernel(got_far, got_near, far, near, wt, kv, fc_ref, ft_ref, ff_ref, ext):
    odd = lax.rem(lax.axis_index("tile"), 2)
    pad6 = jnp.zeros((SUB - BANDS, LANES), F32)
    for base, part in ((24 - 24 * odd, got_near), (24 * odd, got_far), (16 - 8 * odd, near), (8 + 8 * odd, far)):
        for r in range(8):
            ext[base + r] = jnp.concatenate([part[pl.ds(r * BANDS, BANDS), :], pad6], axis=0)
    z = jnp.zeros((32, LANES), BF)
    for r in range(16):
        f = kv[0] * ext[r]
        for t in range(1, TAPS):
            f = f + kv[t] * ext[r + t]
        w = jnp.concatenate([wt[pl.ds(r, BANDS, stride=16), :], pad6], axis=0)
        wf = w * f
        ff_ref[pl.ds(r, 1), :] = jnp.sum(wf * f, axis=0, keepdims=True)
        at = pl.ds((r % 2) * LANES, LANES)
        for ref, x in ((fc_ref, wf * SCALE), (ft_ref, w)):
            a, b, c = split3(x)
            ref[r // 2, :, at] = jnp.concatenate([a, b, a, c, b, a, z], axis=0)


def rows(got_far, got_near, far, near, wt, kv):
    vm = pl.BlockSpec(memory_space=pltpu.VMEM)
    side = pltpu.VMEM((8, LANES, 2 * LANES), BF)
    return pl.pallas_call(
        rows_kernel,
        out_shape=(side, side, pltpu.VMEM((16, LANES), F32)),
        in_specs=[vm] * 6,
        out_specs=(vm,) * 3,
        scratch_shapes=[pltpu.VMEM((32, SUB, LANES), F32)],
        name="rows",
    )(on_chip(got_far), on_chip(got_near), on_chip(far), on_chip(near), on_chip(wt.reshape(BANDS * 16, LANES)), on_chip(kv))


def fit_kernel(fc_ref, ft_ref, ff_ref, bank, pm_ref, le_ref, lc, lt, cs, g_ref, e_ref, *, R, L, NS, S, PR):
    refs = (fc_ref, ft_ref, ff_ref, bank, pm_ref, le_ref, lc, lt, cs, g_ref, e_ref)
    pl.run_scoped(
        functools.partial(fit_body, *refs, R=R, L=L, S=S, PR=PR),
        pltpu.ACC(0)((SUB, 256), F32),
        pltpu.ACC(1)((SUB, 256), F32),
        *[pltpu.ACC(0)((R, 256), F32) for _ in range(NS)],
        *[pltpu.ACC(1)((R, 256), F32) for _ in range(NS)],
    )


def fit_body(
    fc_ref, ft_ref, ff_ref, bank, pm_ref, le_ref, lc, lt, cs, g_ref, e_ref, acc_e0, acc_e1, *accs, R, L, S, PR
):
    NS = len(accs) // 2
    acc_c, acc_t = accs[:NS], accs[NS:]
    row16 = lax.broadcasted_iota(jnp.int32, (SUB, LANES), 0)
    NT = lc.shape[0]
    KC = 256
    n1 = NT // KC
    G = KC // R
    NG = NT // R
    zl = jnp.zeros((R, LANES), BF)
    zs = jnp.zeros((SUB, LANES), BF)
    ze = jnp.zeros((LANES, 2 * LANES), BF)

    def lhs_prep(s):
        zeros32 = jnp.zeros((32, LANES), F32)
        blk = bank[s]
        T = jnp.where(row16 < BANDS, blk, 0.0)
        for dst, X in ((lc, T), (lt, T * T)):
            a, b, c = (v.astype(F32) for v in split3(X))
            st = jnp.concatenate([a, a, b, a, b, c, zeros32], axis=0)
            dst[pl.ds(s * LANES, LANES), :] = st.T.astype(BF)
        cc = (2.0 * blk + 1.0) * (1.0 / 128.0)
        cc = jnp.where(row16 == 13, 1.0, jnp.where((row16 >= 10) & (row16 < 13), cc, 0.0))
        cs[:, pl.ds(s * LANES, LANES)] = cc.astype(BF)

    def push(i, tile, stage):
        for mxu, side in enumerate((fc_ref, ft_ref)):
            e = ze if tile is None else e_ref[pl.ds(tile * KC + mxu * LANES, LANES), :]
            pltpu.matmul_push_rhs(jnp.concatenate([side[i], e], axis=0), stage, mxu)

    def issue(q, stage):
        for acc, src in ((acc_c, lc), (acc_t, lt)):
            pltpu.matmul_acc_lhs(acc[q % NS], jnp.concatenate([src[pl.ds(q * R, R), :], zl], axis=1), load_staged_rhs=stage)

    def edot(tile, stage=None):
        for mxu, acc in enumerate((acc_e0, acc_e1)):
            lhs = jnp.concatenate([zs, cs[:, pl.ds(tile * KC + mxu * LANES, LANES)]], axis=1)
            pltpu.matmul_acc_lhs(acc, lhs, load_staged_rhs=stage)

    def take(q, m):
        c = pltpu.matmul_pop(acc_c[q % NS])
        t = pltpu.matmul_pop(acc_t[q % NS])
        g = c * c / t
        g_ref[pl.ds(q * R, R), :] = g
        mm = jnp.max(g.reshape(R // 8, 8, 256), axis=0)
        return mm if m is None else jnp.maximum(m, mm)

    def exps(q, m):
        rows = pl.ds(q * R, R)
        e_ref[rows, :] = jnp.exp2(g_ref[rows, :] - m).astype(BF)

    def finish(r2, m):
        acc = pltpu.matmul_pop(acc_e0) + pltpu.matmul_pop(acc_e1)
        tot = acc[13:14]
        pm = acc[10:13] / tot
        le = m * LN2 + jnp.log(tot)
        for j in range(2):
            sl = slice(j * LANES, j * LANES + LANES)
            at = pl.ds(2 * r2 + j, 1)
            for q in range(3):
                pm_ref[q, at, :] = pm[q : q + 1, sl]
            le_ref[at, :] = le[:, sl] - 0.5 * ff_ref[at, :]

    top = lambda m: jnp.max(m, axis=0, keepdims=True)
    last = 7
    g_ref[pl.ds((NG - L) * R, L * R), :] = jnp.zeros((L * R, 256), F32)
    e_ref[pl.ds((n1 - S) * KC, S * KC), :] = jnp.ones((S * KC, 256), BF)

    push(0, None, 0)
    m = None
    for q in range(NG):
        if q * R % LANES == 0:
            lhs_prep(q * R // LANES)
        issue(q, 0 if q == 0 else None)
        if q >= L:
            m = take(q - L, m)
    push(1, n1 - S, 0)

    def body(i, carry):
        m_before, old = carry
        new = m = None
        for q in range(NG):
            k, r = divmod(q, G)
            issue(q, k % 2 if r == 0 else None)
            if r == 0:
                if k == S:
                    finish(jnp.maximum(i - 2, 0), old)
                edot((k - S) % n1)
            if q < L:
                exps(NG + q - L, old)
            else:
                exps(q - L, new)
            if r == PR:
                step = k + 1
                if step < n1:
                    push(i, (step - S) % n1, step % 2)
                else:
                    push(jnp.minimum(i + 1, last), n1 - S, 0)
            if q < L:
                m_before = take(NG + q - L, m_before)
                if q == L - 1:
                    new = top(m_before)
            else:
                m = take(q - L, m)
        return m, new

    m, old = lax.fori_loop(1, last + 1, body, (m, jnp.zeros((1, 256), F32)))
    for q in range(max(L, S * G)):
        k, r = divmod(q, G)
        if r == 0 and k < S:
            edot(n1 - S + k, k % 2)
        if q < L:
            exps(NG + q - L, old)
        if r == PR and k + 1 < S:
            push(last, n1 - S + k + 1, (k + 1) % 2)
        if q < L:
            m = take(NG + q - L, m)
    finish(last - 1, old)
    new = top(m)
    for k in range(n1):
        for r in range(G):
            exps(k * G + r, new)
        push(last, k, (S + k) % 2)
        edot(k, (S + k) % 2)
    finish(last, new)


def fit(fc, ft, ff, bank, R=64, NS=8, L=7, S=3, PR=3):
    vm = pl.BlockSpec(memory_space=pltpu.VMEM)
    nt = bank.shape[0] * LANES
    return pl.pallas_call(
        functools.partial(fit_kernel, R=R, L=L, NS=NS, S=S, PR=PR),
        out_shape=(jax.ShapeDtypeStruct((3, 16, LANES), F32), jax.ShapeDtypeStruct((16, LANES), F32)),
        in_specs=[vm] * 4,
        out_specs=(vm, vm),
        scratch_shapes=[
            pltpu.VMEM((nt, LANES), BF),
            pltpu.VMEM((nt, LANES), BF),
            pltpu.VMEM((SUB, nt), BF),
            pltpu.VMEM((nt, 256), F32),
            pltpu.VMEM((nt, 256), BF),
        ],
        name="fit",
    )(on_chip(fc), on_chip(ft), on_chip(ff), on_chip(bank))


def swaps(start, count):
    pairs = [(i, i + 1) for i in range(start, count - 1, 2)]
    return pairs + [(j, i) for i, j in pairs]


def body(sky_image, inverse_var, kernel_taps, kernel_sizes, templates, grid_index):
    shards = lax.axis_size("tmpl")
    tiles = lax.axis_size("tile")
    bank, cols, weight, kv = head(sky_image, inverse_var, kernel_taps, kernel_sizes, templates, grid_index, shards)
    bank = lax.all_to_all(bank, "tmpl", split_axis=0, concat_axis=0, tiled=True)
    far, near = columns(cols, kv, shards)
    got_far = lax.ppermute(far, "tile", swaps(1, tiles))
    got_near = lax.ppermute(near, "tile", swaps(0, tiles))
    fc, ft, ff = rows(got_far, got_near, far, near, weight, kv)
    return fit(fc, ft, ff, bank)


def solution(mesh):
    placed = (
        P(None, "tile", None),
        P(None, "tile", None),
        P(),
        P(),
        P(None, "tmpl"),
        P(None, "tmpl"),
    )
    return jax.shard_map(
        body,
        mesh=mesh,
        in_specs=placed,
        out_specs=(P(None, "tile", "tmpl"), P("tile", "tmpl")),
        check_vma=False,
    )
```

```python
import functools
import math

import jax
import jax.numpy as jnp
from jax import lax
from jax.experimental import pallas as pl
from jax.experimental.pallas import tpu as pltpu
from jax.sharding import PartitionSpec as P

BANDS = 10
RADIUS = 8
TAPS = 2 * RADIUS + 1
LANES = 128
SUB = 16
SCALE = math.sqrt(0.5 / math.log(2.0))
LN2 = math.log(2.0)
BF = jnp.bfloat16
F32 = jnp.float32


def head_kernel(
    sky, ivar, taps, sizes, templates, grid_index, bank, cols, weight, kv, rows, gi, tk, sz, sems, bank_sems
):
    c = lax.axis_index("tmpl")
    shards = bank.shape[0]
    at = lambda i: pl.ds(pl.multiple_of(i * LANES, LANES), LANES)
    reads = [
        pltpu.make_async_copy(templates, rows.at[0:BANDS], sems.at[0]),
        pltpu.make_async_copy(grid_index, gi, sems.at[1]),
        pltpu.make_async_copy(taps, tk, sems.at[2]),
        pltpu.make_async_copy(sizes, sz, sems.at[3]),
        pltpu.make_async_copy(sky.at[:, :, at(jnp.maximum(c - 1, 0))], cols.at[0], sems.at[4]),
        pltpu.make_async_copy(sky.at[:, :, at(c)], cols.at[1], sems.at[5]),
        pltpu.make_async_copy(sky.at[:, :, at(jnp.minimum(c + 1, shards - 1))], cols.at[2], sems.at[6]),
        pltpu.make_async_copy(ivar.at[:, :, at(c)], weight, sems.at[7]),
    ]
    for copy in reads:
        copy.start()
    rows[BANDS + 3 : SUB] = jnp.zeros((SUB - BANDS - 3, LANES), F32)
    reads[1].wait()
    rows[BANDS : BANDS + 3] = gi[...].astype(F32)
    reads[0].wait()
    writes = [pltpu.make_async_copy(rows, bank.at[s], bank_sems.at[s]) for s in range(shards)]
    for copy in writes:
        copy.start()
    reads[2].wait()
    reads[3].wait()
    band = lax.broadcasted_iota(jnp.int32, (BANDS, TAPS), 0)
    tap = lax.broadcasted_iota(jnp.int32, (BANDS, TAPS), 1)
    half = jnp.zeros((BANDS, TAPS), jnp.int32)
    for b in range(BANDS):
        half = jnp.where(band == b, sz[b], half)
    kern = jnp.where(jnp.abs(tap - RADIUS) <= half, tk[...], 0.0)
    kern = kern / jnp.sum(kern, axis=1, keepdims=True)
    for t in range(TAPS):
        kv[t, 0:BANDS] = jnp.broadcast_to(kern[:, t : t + 1], (BANDS, LANES))
        kv[t, BANDS:SUB] = jnp.zeros((SUB - BANDS, LANES), F32)
    for copy in reads[4:]:
        copy.wait()
    for copy in writes:
        copy.wait()


def head(sky, ivar, taps, sizes, templates, grid_index, shards):
    hbm = pl.BlockSpec(memory_space=pl.ANY)
    vm = pl.BlockSpec(memory_space=pltpu.VMEM)
    return pl.pallas_call(
        head_kernel,
        out_shape=(
            jax.ShapeDtypeStruct((shards, SUB, LANES), F32),
            pltpu.VMEM((3, BANDS, 16, LANES), F32),
            pltpu.VMEM((BANDS, 16, LANES), F32),
            pltpu.VMEM((TAPS, SUB, LANES), F32),
        ),
        in_specs=[hbm] * 6,
        out_specs=(hbm, vm, vm, vm),
        scratch_shapes=[
            pltpu.VMEM((SUB, LANES), F32),
            pltpu.VMEM((3, LANES), jnp.int32),
            pltpu.VMEM((BANDS, TAPS), F32),
            pltpu.SMEM((BANDS,), jnp.int32),
            pltpu.SemaphoreType.DMA((8,)),
            pltpu.SemaphoreType.DMA((shards,)),
        ],
        name="head",
    )(sky, ivar, taps, sizes, templates, grid_index)


def columns_kernel(cols, kv, far, near, *, shards):
    c = lax.axis_index("tmpl")
    odd = lax.rem(lax.axis_index("tile"), 2) == 1
    lane = lax.broadcasted_iota(jnp.int32, (16, LANES), 1)
    right_ok = jnp.where(c < shards - 1, 1.0, 0.0)
    left_ok = jnp.where(c > 0, 1.0, 0.0)
    for b in range(BANDS):
        main = cols[1, b]
        side = jnp.where(lane < LANES // 2, cols[2, b] * right_ok, cols[0, b] * left_ok)
        tap = lambda t: jnp.broadcast_to(kv[t, b : b + 1, :], (16, LANES))
        acc = main * tap(RADIUS)
        for d in range(1, RADIUS + 1):
            up = pltpu.roll(jnp.where(lane >= d, main, side), LANES - d, 1)
            down = pltpu.roll(jnp.where(lane < LANES - d, main, side), d, 1)
            acc = acc + up * tap(RADIUS + d)
            acc = acc + down * tap(RADIUS - d)
        far[pl.ds(b, 8, stride=BANDS), :] = jnp.where(odd, acc[8:], acc[:8])
        near[pl.ds(b, 8, stride=BANDS), :] = jnp.where(odd, acc[:8], acc[8:])


def on_chip(x):
    return pltpu.with_memory_space_constraint(x, pltpu.VMEM)


def columns(cols, kv, shards):
    vm = pl.BlockSpec(memory_space=pltpu.VMEM)
    part = pltpu.VMEM((8 * BANDS, LANES), F32)
    return pl.pallas_call(
        functools.partial(columns_kernel, shards=shards),
        out_shape=(part, part),
        in_specs=[vm] * 2,
        out_specs=(vm,) * 2,
        name="columns",
    )(on_chip(cols), on_chip(kv))


def split3(x):
    a = x.astype(BF)
    r = x - a.astype(F32)
    b = r.astype(BF)
    r = r - b.astype(F32)
    return a, b, r.astype(BF)


def rows_kernel(got_far, got_near, far, near, wt, kv, fc_ref, ft_ref, ff_ref, ext):
    odd = lax.rem(lax.axis_index("tile"), 2)
    pad6 = jnp.zeros((SUB - BANDS, LANES), F32)
    for base, part in ((24 - 24 * odd, got_near), (24 * odd, got_far), (16 - 8 * odd, near), (8 + 8 * odd, far)):
        for r in range(8):
            ext[base + r] = jnp.concatenate([part[pl.ds(r * BANDS, BANDS), :], pad6], axis=0)
    z = jnp.zeros((32, LANES), BF)
    for r in range(16):
        f = kv[0] * ext[r]
        for t in range(1, TAPS):
            f = f + kv[t] * ext[r + t]
        w = jnp.concatenate([wt[pl.ds(r, BANDS, stride=16), :], pad6], axis=0)
        wf = w * f
        ff_ref[pl.ds(r, 1), :] = jnp.sum(wf * f, axis=0, keepdims=True)
        at = pl.ds((r % 2) * LANES, LANES)
        for ref, x in ((fc_ref, wf * SCALE), (ft_ref, w)):
            a, b, c = split3(x)
            ref[r // 2, :, at] = jnp.concatenate([a, b, a, c, b, a, z], axis=0)


def rows(got_far, got_near, far, near, wt, kv):
    vm = pl.BlockSpec(memory_space=pltpu.VMEM)
    side = pltpu.VMEM((8, LANES, 2 * LANES), BF)
    return pl.pallas_call(
        rows_kernel,
        out_shape=(side, side, pltpu.VMEM((16, LANES), F32)),
        in_specs=[vm] * 6,
        out_specs=(vm,) * 3,
        scratch_shapes=[pltpu.VMEM((32, SUB, LANES), F32)],
        name="rows",
    )(on_chip(got_far), on_chip(got_near), on_chip(far), on_chip(near), on_chip(wt.reshape(BANDS * 16, LANES)), on_chip(kv))


def fit_kernel(fc_ref, ft_ref, ff_ref, bank, pm_ref, le_ref, lc, lt, cs, g_ref, e_ref, *, R, L, NS, S, PR):
    refs = (fc_ref, ft_ref, ff_ref, bank, pm_ref, le_ref, lc, lt, cs, g_ref, e_ref)
    pl.run_scoped(
        functools.partial(fit_body, *refs, R=R, L=L, S=S, PR=PR),
        pltpu.ACC(0)((SUB, 256), F32),
        pltpu.ACC(1)((SUB, 256), F32),
        *[pltpu.ACC(0)((R, 256), F32) for _ in range(NS)],
        *[pltpu.ACC(1)((R, 256), F32) for _ in range(NS)],
    )


def fit_body(
    fc_ref, ft_ref, ff_ref, bank, pm_ref, le_ref, lc, lt, cs, g_ref, e_ref, acc_e0, acc_e1, *accs, R, L, S, PR
):
    NS = len(accs) // 2
    acc_c, acc_t = accs[:NS], accs[NS:]
    row16 = lax.broadcasted_iota(jnp.int32, (SUB, LANES), 0)
    NT = lc.shape[0]
    KC = 2 * R
    n1 = NT // KC
    G = KC // R
    NG = NT // R
    zl = jnp.zeros((R, LANES), BF)
    zs = jnp.zeros((SUB, LANES), BF)
    ze = jnp.zeros((LANES, 2 * LANES), BF)

    def lhs_prep(s):
        zeros32 = jnp.zeros((32, LANES), F32)
        blk = bank[s]
        T = jnp.where(row16 < BANDS, blk, 0.0)
        for dst, X in ((lc, T), (lt, T * T)):
            a, b, c = (v.astype(F32) for v in split3(X))
            st = jnp.concatenate([a, a, b, a, b, c, zeros32], axis=0)
            dst[pl.ds(s * LANES, LANES), :] = st.T.astype(BF)
        cc = (2.0 * blk + 1.0) * (1.0 / 128.0)
        cc = jnp.where(row16 == 13, 1.0, jnp.where((row16 >= 10) & (row16 < 13), cc, 0.0))
        cc = cc.astype(BF)
        for h in range(2):
            half = cc[:, h * R : h * R + R]
            cs[:, pl.ds((2 * s + h) * LANES, LANES)] = jnp.concatenate([half, half], axis=1)

    def push(i, tile, stage):
        for mxu, side in enumerate((fc_ref, ft_ref)):
            e = ze if tile is None else e_ref[pl.ds((2 * tile + mxu) * LANES, LANES), :]
            pltpu.matmul_push_rhs(jnp.concatenate([side[i], e], axis=0), stage, mxu)

    def issue(q, stage):
        for acc, src in ((acc_c, lc), (acc_t, lt)):
            pltpu.matmul_acc_lhs(acc[q % NS], jnp.concatenate([src[pl.ds(q * R, R), :], zl], axis=1), load_staged_rhs=stage)

    def edot(tile, stage=None):
        for mxu, acc in enumerate((acc_e0, acc_e1)):
            lhs = jnp.concatenate([zs, cs[:, pl.ds((2 * tile + mxu) * LANES, LANES)]], axis=1)
            pltpu.matmul_acc_lhs(acc, lhs, load_staged_rhs=stage)

    def take(q, m):
        c = pltpu.matmul_pop(acc_c[q % NS])
        t = pltpu.matmul_pop(acc_t[q % NS])
        g = c * c / t
        g_ref[pl.ds(q * R, R), :] = g
        mm = jnp.max(g.reshape(R // 8, 8, 256), axis=0)
        return mm if m is None else jnp.maximum(m, mm)

    def exps(q, m):
        rows = pl.ds(q * R, R)
        e = jnp.exp2(g_ref[rows, :] - m)
        hi = e.astype(BF)
        e_ref[pl.ds(q * LANES, R), :] = hi
        e_ref[pl.ds(q * LANES + R, R), :] = (e - hi.astype(F32)).astype(BF)

    def finish(r2, m):
        acc = pltpu.matmul_pop(acc_e0) + pltpu.matmul_pop(acc_e1)
        tot = acc[13:14]
        pm = acc[10:13] / tot
        le = m * LN2 + jnp.log(tot)
        for j in range(2):
            sl = slice(j * LANES, j * LANES + LANES)
            at = pl.ds(2 * r2 + j, 1)
            for q in range(3):
                pm_ref[q, at, :] = pm[q : q + 1, sl]
            le_ref[at, :] = le[:, sl] - 0.5 * ff_ref[at, :]

    top = lambda m: jnp.max(m, axis=0, keepdims=True)
    last = 7
    g_ref[pl.ds((NG - L) * R, L * R), :] = jnp.zeros((L * R, 256), F32)
    e_ref[pl.ds((n1 - S) * 2 * LANES, S * 2 * LANES), :] = jnp.ones((S * 2 * LANES, 256), BF)

    push(0, None, 0)
    m = None
    for q in range(NG):
        if q * R % LANES == 0:
            lhs_prep(q * R // LANES)
        issue(q, 0 if q == 0 else None)
        if q >= L:
            m = take(q - L, m)
    push(1, n1 - S, 0)

    def body(i, carry):
        m_before, old = carry
        new = m = None
        for q in range(NG):
            k, r = divmod(q, G)
            issue(q, k % 2 if r == 0 else None)
            if r == 0:
                if k == S:
                    finish(jnp.maximum(i - 2, 0), old)
                edot((k - S) % n1)
            if q < L:
                exps(NG + q - L, old)
            else:
                exps(q - L, new)
            if r == PR:
                step = k + 1
                if step < n1:
                    push(i, (step - S) % n1, step % 2)
                else:
                    push(jnp.minimum(i + 1, last), n1 - S, 0)
            if q < L:
                m_before = take(NG + q - L, m_before)
                if q == L - 1:
                    new = top(m_before)
            else:
                m = take(q - L, m)
        return m, new

    m, old = lax.fori_loop(1, last + 1, body, (m, jnp.zeros((1, 256), F32)))
    for q in range(max(L, S * G)):
        k, r = divmod(q, G)
        if r == 0 and k < S:
            edot(n1 - S + k, k % 2)
        if q < L:
            exps(NG + q - L, old)
        if r == PR and k + 1 < S:
            push(last, n1 - S + k + 1, (k + 1) % 2)
        if q < L:
            m = take(NG + q - L, m)
    finish(last - 1, old)
    new = top(m)
    for k in range(n1):
        for r in range(G):
            exps(k * G + r, new)
        push(last, k, (S + k) % 2)
        edot(k, (S + k) % 2)
    finish(last, new)


def fit(fc, ft, ff, bank, R=64, NS=8, L=7, S=5, PR=1):
    vm = pl.BlockSpec(memory_space=pltpu.VMEM)
    nt = bank.shape[0] * LANES
    return pl.pallas_call(
        functools.partial(fit_kernel, R=R, L=L, NS=NS, S=S, PR=PR),
        out_shape=(jax.ShapeDtypeStruct((3, 16, LANES), F32), jax.ShapeDtypeStruct((16, LANES), F32)),
        in_specs=[vm] * 4,
        out_specs=(vm, vm),
        scratch_shapes=[
            pltpu.VMEM((nt, LANES), BF),
            pltpu.VMEM((nt, LANES), BF),
            pltpu.VMEM((SUB, 2 * nt), BF),
            pltpu.VMEM((nt, 256), F32),
            pltpu.VMEM((2 * nt, 256), BF),
        ],
        name="fit",
    )(on_chip(fc), on_chip(ft), on_chip(ff), on_chip(bank))


def swaps(start, count):
    pairs = [(i, i + 1) for i in range(start, count - 1, 2)]
    return pairs + [(j, i) for i, j in pairs]


def body(sky_image, inverse_var, kernel_taps, kernel_sizes, templates, grid_index):
    shards = lax.axis_size("tmpl")
    tiles = lax.axis_size("tile")
    bank, cols, weight, kv = head(sky_image, inverse_var, kernel_taps, kernel_sizes, templates, grid_index, shards)
    bank = lax.all_to_all(bank, "tmpl", split_axis=0, concat_axis=0, tiled=True)
    far, near = columns(cols, kv, shards)
    got_far = lax.ppermute(far, "tile", swaps(1, tiles))
    got_near = lax.ppermute(near, "tile", swaps(0, tiles))
    fc, ft, ff = rows(got_far, got_near, far, near, weight, kv)
    return fit(fc, ft, ff, bank)


def solution(mesh):
    placed = (
        P(None, "tile", None),
        P(None, "tile", None),
        P(),
        P(),
        P(None, "tmpl"),
        P(None, "tmpl"),
    )
    return jax.shard_map(
        body,
        mesh=mesh,
        in_specs=placed,
        out_specs=(P(None, "tile", "tmpl"), P("tile", "tmpl")),
        check_vma=False,
    )
```
